1024 devices in a mesh: section: 64 (over z, core), tensor: 16 (over x, y).
Axes of the slice: x: 4, y: 4, z: 32, core: 2. Of those that a mesh axis runs over, the one named last changes fastest.
Arguments:
- section_inputs: bfloat16 [64, 2, 8192, 128], P('section', None, 'tensor'), may hold values from -6 to 6
- arriving_grad: bfloat16 [64, 8192, 128], P('section', 'tensor'), may hold values from -1.5 to 1.5
- loss_grad: bfloat16 [1, 8192, 128], P(None, 'tensor'), may hold values from -1.5 to 1.5
- factor_first: bfloat16 [64, 3, 64, 128, 128], P('section', None, 'tensor'), may hold values from -0.5 to 0.5
- factor_second: bfloat16 [64, 3, 64, 128, 128], P('section', None, 'tensor'), may hold values from -0.5 to 0.5
- gate_scales: float32 [64, 3, 8192], P('section', None, 'tensor'), may hold values from 0.25 to 1.5
- layer_count: int32 [64], P('section'), may hold values from 1 to 3, as said below
Outputs:
- last_emitted: bfloat16 [64, 8192, 128], P('section', 'tensor')
- factor_first_grad: bfloat16 [64, 3, 64, 128, 128], P('section', None, 'tensor')
- factor_second_grad: bfloat16 [64, 3, 64, 128, 128], P('section', None, 'tensor')
- gate_grad: float32 [64, 3, 8192], P('section', None, 'tensor')
The draws below stay inside these ranges and needn't reach their ends.
Inputs may be any that keep to these rules, and one draw needn't show every extreme that they name: `layer_count`: every section runs at least one layer and some section runs 3.
All inputs are finite; a program needn't handle non-finite values.
Results may differ from the reference program's by a relative error of at most 0.017.
Values may be sent and summed in bfloat16 or wider, within the bound.
No kernel may reach another device: no remote copies, remote signals or barrier semaphores. Data moves between devices by JAX's collectives and lax.ppermute only.
A program may use at most 32 MiB of HBM per device.

```python
import jax
import jax.numpy as jnp
from jax import lax

NB = 64
BS = 128
D = 8192
LMAX = 3
TICKS = 2
TOK = 128
SECTIONS = 64


def draw_layer_count(key, part):
    first_key, second_key = jax.random.split(key)
    counts = jax.random.randint(first_key, (SECTIONS,), 1, 3)
    heavy_sections = jax.random.permutation(second_key, SECTIONS)[:SECTIONS // 16 + 1]
    counts = counts.at[heavy_sections].set(LMAX)
    return counts.astype(jnp.int32)


def block_scale(stream_key, extent, shards, low, high):
    factor_of, own = 1.0, jax.random.fold_in(stream_key, 6)
    for position, shards_of in shards:
        steps = jnp.exp(jax.random.uniform(jax.random.fold_in(own, position), (shards_of,), jnp.float32, low / len(shards), high / len(shards)))
        factor_of = factor_of * jnp.repeat(steps, extent[position] // shards_of).reshape([-1 if axis == position else 1 for axis in range(len(extent))])
    return factor_of


def noise(rng, shape, deviation, bound, cuts=(), dtype=jnp.bfloat16):
    factor_of = block_scale(rng, shape, cuts, -0.22, 0.18) if cuts else 1.0
    array = jax.random.normal(rng, shape, jnp.float32) * deviation * factor_of
    return jnp.minimum(jnp.maximum(array, -bound), bound).astype(dtype)


def setup_inputs(seed: int = 0) -> dict:
    seeds = jax.random.split(jax.random.key(seed), 8)
    section_inputs = noise(seeds[0], (SECTIONS, TICKS, D, TOK), 1.0, 6.0, ((0, 64), (2, 16)))
    arriving_grad = noise(seeds[1], (SECTIONS, D, TOK), 0.25, 1.5, ((0, 64), (1, 16)))
    loss_grad = noise(seeds[2], (TICKS - 1, D, TOK), 0.25, 1.5, ((1, 16),))
    factor_first = noise(seeds[3], (SECTIONS, LMAX, NB, BS, BS), BS ** -0.5, 0.5, ((0, 64), (2, 16)))
    factor_second = noise(seeds[4], (SECTIONS, LMAX, NB, BS, BS), BS ** -0.5, 0.5, ((0, 64), (2, 16)))
    gate_scales = jnp.clip(0.25 + 1.25 * jax.random.uniform(seeds[5], (SECTIONS, LMAX, D), jnp.float32) ** block_scale(seeds[5], (SECTIONS, LMAX, D), ((0, 64), (2, 16)), -0.2, 0.2), 0.25, 1.5)
    layer_count = draw_layer_count(jax.random.fold_in(seeds[7], 71), 0)
    return dict(section_inputs=section_inputs, arriving_grad=arriving_grad, loss_grad=loss_grad, factor_first=factor_first, factor_second=factor_second, gate_scales=gate_scales, layer_count=layer_count)


def permute_blocks(values):
    blocks_all = values.shape[0]
    repeat_count = values.shape[1] // blocks_all
    grid = values.reshape(blocks_all, blocks_all, repeat_count, -1).transpose(1, 2, 0, 3)
    return grid.reshape(blocks_all, blocks_all * repeat_count, -1)


def unpermute_blocks(values):
    blocks_all = values.shape[0]
    repeat_count = values.shape[1] // blocks_all
    grid = values.reshape(blocks_all, repeat_count, blocks_all, -1).transpose(2, 0, 1, 3)
    return grid.reshape(blocks_all, blocks_all * repeat_count, -1)


def apply_blocks(factor, values):
    return jnp.einsum("kij,kjt->kit", factor.astype(jnp.float32), values.astype(jnp.float32))


def apply_transposed(factor, values):
    return jnp.einsum("kji,kjt->kit", factor.astype(jnp.float32), values.astype(jnp.float32))


def section_backward(initial, grad_in, factor_one, factor_two, gate_rows, layer_total):
    hidden = initial.reshape(NB, BS, TOK)
    saved = []
    for layer_slot in range(LMAX):
        first_out = apply_blocks(factor_one[layer_slot], hidden).astype(jnp.bfloat16)
        permuted = permute_blocks(first_out)
        mixed = apply_blocks(factor_two[layer_slot], permuted)
        gate_now = gate_rows[layer_slot].reshape(NB, BS, 1)
        next_hidden = (hidden.astype(jnp.float32) + gate_now * (mixed * jax.nn.sigmoid(mixed))).astype(jnp.bfloat16)
        saved.append((hidden, permuted, mixed))
        hidden = jnp.where(layer_slot < layer_total, next_hidden, hidden)
    grad_now = grad_in.reshape(NB, BS, TOK).astype(jnp.float32)
    first_terms = [None] * LMAX
    second_terms = [None] * LMAX
    gate_terms = [None] * LMAX
    for layer_slot in reversed(range(LMAX)):
        hidden, permuted, mixed = saved[layer_slot]
        is_live = layer_slot < layer_total
        logistic = jax.nn.sigmoid(mixed)
        gate_now = gate_rows[layer_slot].reshape(NB, BS, 1)
        gate_term = jnp.sum(grad_now * (mixed * logistic), axis=2)
        scaled = (grad_now * gate_now * logistic * (1.0 + mixed * (1.0 - logistic))).astype(jnp.bfloat16)
        backed = apply_transposed(factor_two[layer_slot], scaled).astype(jnp.bfloat16)
        returned = unpermute_blocks(backed)
        second_term = jnp.einsum("kit,kjt->kij", scaled.astype(jnp.float32), permuted.astype(jnp.float32))
        first_term = jnp.einsum("kit,kjt->kij", returned.astype(jnp.float32), hidden.astype(jnp.float32))
        moved_grad = grad_now + apply_transposed(factor_one[layer_slot], returned)
        grad_now = jnp.where(is_live, moved_grad, grad_now)
        first_terms[layer_slot] = jnp.where(is_live, first_term, jnp.zeros_like(first_term))
        second_terms[layer_slot] = jnp.where(is_live, second_term, jnp.zeros_like(second_term))
        gate_terms[layer_slot] = jnp.where(is_live, gate_term, jnp.zeros_like(gate_term)).reshape(NB * BS)
    emitted = grad_now.astype(jnp.bfloat16).reshape(NB * BS, TOK)
    return emitted, jnp.stack(first_terms), jnp.stack(second_terms), jnp.stack(gate_terms)


def reference(section_inputs, arriving_grad, loss_grad, factor_first, factor_second, gate_scales, layer_count):
    def emit_only(section_item):
        return section_backward(*section_item)[0]

    grad_list = []
    emitted = None
    for moment in range(TICKS):
        if moment == 0:
            arriving = arriving_grad
        else:
            arriving = jnp.concatenate([emitted[1:], loss_grad[moment - 1][None]], axis=0)
        grad_list.append(arriving)
        emitted = lax.map(emit_only, (section_inputs[:, moment], arriving, factor_first, factor_second, gate_scales, layer_count))
    arrivals = jnp.stack(grad_list, axis=1)

    def section_grads(section_item):
        section_acts, section_arrivals, first_section, second_section, gate_section, total_section = section_item
        sums = None
        for moment in range(TICKS):
            fresh = section_backward(section_acts[moment], section_arrivals[moment], first_section, second_section, gate_section, total_section)[1:]
            if sums is None:
                sums = fresh
            else:
                sums = tuple(older + newer for older, newer in zip(sums, fresh))
        return sums[0].astype(jnp.bfloat16), sums[1].astype(jnp.bfloat16), sums[2]

    first_grad, second_grad, gate_grad = lax.map(section_grads, (section_inputs, arrivals, factor_first, factor_second, gate_scales, layer_count))
    return emitted, first_grad, second_grad, gate_grad
```

```python
import jax
import jax.numpy as jnp
from jax import lax
from jax.experimental import pallas as pl
from jax.experimental.pallas import tpu as pltpu
from jax.sharding import PartitionSpec as P

F32 = jnp.float32
BF16 = jnp.bfloat16


def call(body, name, h_in=(), v_in=(), pins=(), v_out=(), h_out=(), into=(), chain=False):
    vmem = pl.BlockSpec(memory_space=pltpu.VMEM)
    hbm = pl.BlockSpec(memory_space=pltpu.HBM)
    arrays = [item[0] if isinstance(item, tuple) else item for item in h_in]
    places = [item[1] if isinstance(item, tuple) else () for item in h_in]
    shapes = [item[0] if isinstance(item, tuple) else item for item in h_out]
    targets = [item[1] if isinstance(item, tuple) else () for item in h_out]
    loads = [pltpu.VMEM(a.shape[len(p) :], a.dtype) for a, p in zip(arrays, places)]
    stores = [pltpu.VMEM(a.shape[len(p) :], a.dtype) for a, p in zip(shapes, targets)]
    pins = [*pins, *(array for _, array in into)]
    ahead = len(arrays) + len(v_in) + len(pins) - len(into)
    alias = {ahead + k: len(v_out) + number for k, (number, _) in enumerate(into)}
    arrays = [pltpu.with_memory_space_constraint(a, pltpu.HBM) for a in arrays]
    pins = [pltpu.with_memory_space_constraint(a, pltpu.HBM) for a in pins]
    inputs = (*arrays, *v_in, *pins)

    def at(ref, place):
        return ref.at[place] if place else ref

    def kernel(*refs):
        sources, refs = refs[: len(arrays)], refs[len(arrays) :]
        views, refs = refs[: len(v_in)], refs[len(v_in) + len(pins) :]
        results, refs = refs[: len(v_out)], refs[len(v_out) :]
        sinks, refs = refs[: len(shapes)], refs[len(shapes) :]
        loaded, refs = refs[: len(loads)], refs[len(loads) :]
        staged, refs = refs[: len(stores)], refs[len(stores) :]
        in_sems, out_sems = refs
        copies = [
            pltpu.make_async_copy(at(source, place), buffer, in_sems.at[number])
            for number, (source, place, buffer) in enumerate(zip(sources, places, loaded))
        ]
        for copy in copies:
            copy.start()
        pending = []

        def emit(number, value, ref=None):
            if ref is None:
                ref = staged[number]
                ref[...] = value
            copy = pltpu.make_async_copy(ref, at(sinks[number], targets[number]), out_sems.at[number])
            copy.start()
            pending.append(copy)

        waited = set()

        def load(number):
            if number not in waited:
                waited.add(number)
                copies[number].wait()
            return loaded[number]

        body(emit, load, views, results)
        for copy in pending:
            copy.wait()

    moved = sum(a.size * a.dtype.itemsize for a in (*arrays, *v_in, *v_out, *shapes))
    moved = moved if chain else 1024
    return pl.pallas_call(
        kernel,
        out_shape=[*v_out, *(pltpu.HBM(a.shape, a.dtype) for a in shapes)],
        in_specs=[hbm] * len(arrays) + [vmem] * len(v_in) + [hbm] * len(pins),
        out_specs=[vmem] * len(v_out) + [hbm] * len(shapes),
        scratch_shapes=[
            *loads,
            *stores,
            pltpu.SemaphoreType.DMA((max(1, len(loads)),)),
            pltpu.SemaphoreType.DMA((max(1, len(stores)),)),
        ],
        input_output_aliases=alias,
        name=name,
        compiler_params=pltpu.CompilerParams(vmem_limit_bytes=16 << 20),
        cost_estimate=pl.CostEstimate(flops=0, bytes_accessed=moved, transcendentals=0),
    )(*inputs)


def merged(name, tasks, pins=()):
    sources, keys, plans = [], {}, []
    v_out, h_out, into = [], [], []
    for body, needs, shows, keeps, fills in tasks:
        numbers = []
        for item in needs:
            array, place = item if isinstance(item, tuple) else (item, ())
            key = (id(array), place)
            if key not in keys:
                keys[key] = len(sources)
                sources.append((array, place))
            numbers.append(keys[key])
        plans.append((body, numbers, len(v_out), len(h_out)))
        into += [(number + len(h_out), array) for number, array in fills]
        v_out += shows
        h_out += keeps

    def kernel(emit, load, views, results):
        for body, numbers, shown, kept in plans:
            body(
                lambda number, value: emit(kept + number, value),
                lambda number: load(numbers[number]),
                views,
                results[shown:],
            )

    outs = call(kernel, name, h_in=sources, pins=pins, v_out=v_out, h_out=h_out, into=into)
    split = []
    for (_, _, shown, kept), (_, _, shows, keeps, _) in zip(plans, tasks):
        base = len(v_out) + kept
        split.append([*outs[shown : shown + len(shows)], *outs[base : base + len(keeps)]])
    return split


def dot(left, right):
    return jnp.dot(left, right, preferred_element_type=F32)


def dot_t(left, right):
    return lax.dot_general(left, right, (((1,), (1,)), ((), ())), preferred_element_type=F32)


def one_hot(match):
    return jnp.where(match, 1.0, 0.0).astype(BF16)


def first_rows(sizes, axis):
    blocks, size, parts = sizes
    rows = blocks * size
    each = size // parts
    wire = lax.broadcasted_iota(jnp.int32, (rows, rows), axis)
    natural = lax.broadcasted_iota(jnp.int32, (rows, rows), 1 - axis)
    part = wire // (blocks * each)
    block = (wire // each) % blocks
    return one_hot(natural == block * size + part * each + wire % each)


def second_rows(sizes, axis):
    blocks, size, parts = sizes
    rows = blocks * size
    every = blocks * parts
    repeat = size // every
    wire = lax.broadcasted_iota(jnp.int32, (rows, rows), axis)
    natural = lax.broadcasted_iota(jnp.int32, (rows, rows), 1 - axis)
    source = wire // (blocks * repeat)
    block = (wire // repeat) % blocks
    return one_hot(natural == block * size + (wire % repeat) * every + source)


def sigmoid(values):
    return 1.0 / (1.0 + jnp.exp(-values))


def first_wire(sizes, factor):
    blocks, size, _ = sizes
    order = first_rows(sizes, 0)
    return [
        dot(order[:, block * size : (block + 1) * size], factor[block]).astype(BF16)
        for block in range(blocks)
    ]


def first_back(sizes, factor):
    blocks, size, _ = sizes
    order = first_rows(sizes, 1)
    return [
        dot(
            factor[block].astype(F32).T.astype(BF16), order[block * size : (block + 1) * size]
        ).astype(BF16)
        for block in range(blocks)
    ]


def second_wire(sizes, factor):
    blocks, size, _ = sizes
    order = second_rows(sizes, 1)
    return [
        dot(factor[block], order[block * size : (block + 1) * size]).astype(BF16)
        for block in range(blocks)
    ]


def second_back(sizes, factor):
    blocks, size, _ = sizes
    order = second_rows(sizes, 0)
    return [
        dot(
            order[:, block * size : (block + 1) * size], factor[block].astype(F32).T.astype(BF16)
        ).astype(BF16)
        for block in range(blocks)
    ]


def put_rows(ref, parts):
    size = parts[0].shape[0]
    for number, part in enumerate(parts):
        ref[number * size : (number + 1) * size, :] = part


def put_columns(ref, parts):
    size = parts[0].shape[1]
    for number, part in enumerate(parts):
        ref[:, number * size : (number + 1) * size] = part


def column(row, lanes):
    return jnp.broadcast_to(row, (lanes, row.shape[1])).T


def both(value):
    return jnp.concatenate([value, value], axis=1)


def branch_of(mixed):
    return mixed * sigmoid(mixed)


def slope_of(mixed, gates):
    logistic = sigmoid(mixed)
    return gates * logistic * (1.0 + mixed * (1.0 - logistic))


def exchange(values, parts):
    rows, columns = values.shape
    shaped = values.reshape(parts, rows // parts, columns)
    return lax.all_to_all(shaped, "tensor", 0, 0, tiled=True).reshape(rows, columns)


def shards(
    section_inputs, arriving_grad, loss_grad, factor_first, factor_second, gate_scales, layer_count
):
    slots, blocks, size = factor_first.shape[1:4]
    tokens = section_inputs.shape[3]
    parts = lax.axis_size("tensor")
    sizes = (blocks, size, parts)
    rows = blocks * size
    live = jnp.arange(slots) < layer_count[0]
    gate = jnp.where(live[:, None], gate_scales[0], 0.0)[:, None]
    alive = jnp.where(live[:, None], jnp.ones_like(gate_scales[0]), 0.0)[:, None]
    sections = lax.axis_size("section")
    is_last = lax.axis_index("section") == sections - 1
    loss = jnp.where(is_last, loss_grad[0], jnp.zeros_like(loss_grad[0]))
    last = slots - 1

    def shape(columns, dtype=BF16):
        return jax.ShapeDtypeStruct((rows, columns), dtype)

    wide, slim, square = shape(2 * tokens), shape(tokens), shape(rows)
    wide_f32, slim_f32 = shape(2 * tokens, F32), shape(tokens, F32)
    factor_shape = jax.ShapeDtypeStruct(factor_first.shape, BF16)

    def first_of(slot):
        return (factor_first, (0, slot))

    def second_of(slot):
        return (factor_second, (0, slot))

    def gate_of(slot):
        return (gate, (slot,))

    def open_chain(emit, load, views, results):
        order = first_rows(sizes, 0)
        factor, inputs = load(0), load(1)
        hidden = jnp.concatenate([inputs[0], inputs[1]], axis=1)
        natural = jnp.concatenate(
            [
                dot(factor[block], hidden[block * size : (block + 1) * size]).astype(BF16)
                for block in range(blocks)
            ],
            axis=0,
        )
        emit(0, dot(order, natural).astype(BF16))

    (send,) = call(
        open_chain, "open", h_in=[first_of(0), (section_inputs, (0,))], h_out=[wide], chain=True
    )
    started = section_inputs

    wires, hiddens, mixeds = [], [], []
    for slot in range(last):

        def prepare(emit, load, views, results, slot=slot):
            put_rows(results[0], second_wire(sizes, load(0)))
            put_columns(results[1], first_wire(sizes, load(1)))
            results[2][...] = column(load(2)[...], tokens)
            before = load(3)
            if slot == 0:
                results[3][...] = jnp.concatenate([before[0], before[1]], axis=1)
            else:
                results[3][...] = before[...]

        second_now, first_now, gate_now, hidden = call(
            prepare,
            f"prepare_forward_{slot}",
            h_in=[
                second_of(slot),
                first_of(slot + 1),
                gate_of(slot),
                (section_inputs, (0,)) if slot == 0 else hiddens[-1],
            ],
            pins=[started],
            v_out=[square, square, slim_f32, wide],
        )

        def forward(emit, load, views, results):
            received, hidden, gate_now, second_now, first_now = views
            emit(1, None, received)
            mixed = dot(second_now[...], received[...])
            emit(2, mixed)
            fresh = (hidden[...].astype(F32) + both(gate_now[...]) * branch_of(mixed)).astype(BF16)
            emit(3, fresh)
            emit(0, dot(first_now[...], fresh).astype(BF16))

        send, wire, mixed, fresh = call(
            forward,
            f"forward_{slot}",
            v_in=[exchange(send, parts), hidden, gate_now, second_now, first_now],
            h_out=[wide, wide, wide_f32, wide],
            chain=True,
        )
        wires.append(wire)
        mixeds.append(mixed)
        hiddens.append(fresh)
        started = fresh

    def prepare_turn(emit, load, views, results):
        second = load(0)
        put_rows(results[0], second_wire(sizes, second))
        put_columns(results[1], second_back(sizes, second))
        results[2][...] = column(load(1)[...], tokens)
        results[3][...] = load(2)[...]

    second_now, back_now, gate_now, arriving = call(
        prepare_turn,
        "prepare_turn",
        h_in=[second_of(last), gate_of(last), (arriving_grad, (0,))],
        pins=[started],
        v_out=[square, square, slim_f32, slim],
    )

    def turn(emit, load, views, results):
        received, arriving, gate_now, second_now, back_now = views
        emit(1, None, received)
        mixed = dot(second_now[...], received[...])
        emit(2, mixed)
        slope = slope_of(mixed[:, :tokens], gate_now[...])
        scaled = (arriving[...].astype(F32) * slope).astype(BF16)
        emit(3, scaled)
        emit(0, dot(back_now[...], scaled).astype(BF16))

    send, wire, mixed, scaled = call(
        turn,
        "turn",
        v_in=[exchange(send, parts), arriving, gate_now, second_now, back_now],
        h_out=[slim, wide, wide_f32, slim],
        chain=True,
    )
    wires.append(wire)
    mixeds.append(mixed)
    started = scaled

    scaleds = [[None] * slots, [None] * slots]
    grads = [[None] * slots, [None] * slots]
    returns = [[None] * slots, [None] * slots]
    scaleds[0][last], grads[0][last] = scaled, (arriving_grad, (0,))
    gate_shape = jax.ShapeDtypeStruct(gate.shape, F32)

    def gate_sums(slot, filled):
        def body(emit, load, views, results):
            branch = branch_of(load(0)[...])
            terms = load(1)[...].astype(F32) * branch[:, :tokens]
            terms += load(2)[...].astype(F32) * branch[:, tokens:]
            sums = jnp.sum(terms.T, axis=0, keepdims=True)
            emit(0, jnp.where(load(3)[...] > 0, sums, 0.0))

        return (
            body,
            [mixeds[slot], grads[0][slot], grads[1][slot], (alive, (slot,))],
            [],
            [(gate_shape, (slot,))],
            [] if filled is None else [(0, filled)],
        )

    def second_sums(slot, filled):
        def body(emit, load, views, results):
            order = second_rows(sizes, 1)
            natural = dot(order, load(0)[...]).astype(BF16)
            scaled = jnp.concatenate([load(1)[...], load(2)[...]], axis=1)
            sums = []
            for block in range(blocks):
                span = slice(block * size, (block + 1) * size)
                sums.append(dot_t(scaled[span], natural[span]).astype(BF16))
            emit(0, jnp.stack(sums))

        return (
            body,
            [wires[slot], scaleds[0][slot], scaleds[1][slot]],
            [],
            [(factor_shape, (0, slot))],
            [] if filled is None else [(0, filled)],
        )

    def first_sum(earlier, later, hidden):
        wire = jnp.concatenate([earlier, later], axis=1)
        natural = dot(first_rows(sizes, 1), wire).astype(BF16)
        sums = []
        for block in range(blocks):
            span = slice(block * size, (block + 1) * size)
            sums.append(dot_t(natural[span], hidden[span]).astype(BF16))
        return jnp.stack(sums)

    def first_sums(slot, filled):
        def body(emit, load, views, results):
            emit(0, first_sum(load(0)[...], load(1)[...], load(2)[...]))

        return (
            body,
            [returns[0][slot], returns[1][slot], hiddens[slot - 1]],
            [],
            [(factor_shape, (0, slot))],
            [] if filled is None else [(0, filled)],
        )

    def step(moment, slot, send, started, tasks=()):
        columns = slice(moment * tokens, (moment + 1) * tokens)
        kept = BF16 if slot + 1 == last else F32

        def prepare(emit, load, views, results):
            put_rows(results[0], first_back(sizes, load(0)))
            put_columns(results[1], second_back(sizes, load(1)))
            gates = column(load(2)[...], tokens)
            results[2][...] = slope_of(load(3)[:, columns], gates)
            results[3][...] = load(4)[...]

        task = (
            prepare,
            [
                first_of(slot + 1),
                second_of(slot),
                gate_of(slot),
                mixeds[slot],
                grads[moment][slot + 1],
            ],
            [square, square, slim_f32, shape(tokens, kept)],
            [],
            [],
        )
        ready, *others = merged(f"window_{moment}_{slot}", [task, *tasks], [started])
        first_now, second_now, slope, grad = ready

        def backward(emit, load, views, results):
            received, grad, slope, first_now, second_now = views
            emit(1, None, received)
            grad_now = grad[...].astype(F32) + dot(first_now[...], received[...])
            emit(3, grad_now)
            scaled = (grad_now * slope[...]).astype(BF16)
            emit(2, scaled)
            emit(0, dot(second_now[...], scaled).astype(BF16))

        send, returned, scaled, grad = call(
            backward,
            f"backward_{moment}_{slot}",
            v_in=[exchange(send, parts), grad, slope, first_now, second_now],
            h_out=[slim, slim, slim, slim_f32],
            chain=True,
        )
        returns[moment][slot + 1] = returned
        scaleds[moment][slot] = scaled
        grads[moment][slot] = grad
        return send, scaled, others

    for slot in reversed(range(last)):
        send, started, _ = step(0, slot, send, started)

    def prepare_emit(emit, load, views, results):
        put_rows(results[0], first_back(sizes, load(0)))
        results[1][...] = load(1)[...]

    def prepare_again(emit, load, views, results):
        put_columns(results[0], second_back(sizes, load(0)))
        gates = column(load(1)[...], tokens)
        results[1][...] = slope_of(load(2)[:, tokens:], gates)
        results[2][...] = load(3)[...]

    (first_now, grad), (second_now, slope, loss) = merged(
        "window_emit",
        [
            (prepare_emit, [first_of(0), grads[0][0]], [square, slim_f32], [], []),
            (
                prepare_again,
                [second_of(last), gate_of(last), mixeds[last], loss],
                [square, slim_f32, slim],
                [],
                [],
            ),
        ],
        [started],
    )

    def emit_grad(emit, load, views, results):
        received, grad, first_now = views[:3]
        emit(0, None, received)
        results[0][...] = (grad[...] + dot(first_now[...], received[...])).astype(BF16)

    emitted, returns[0][0] = call(
        emit_grad,
        "emit",
        v_in=[exchange(send, parts), grad, first_now, loss],
        v_out=[slim],
        h_out=[slim],
        chain=True,
    )
    shifted = lax.ppermute(
        emitted, "section", [(source, source - 1) for source in range(1, sections)]
    )

    def again(emit, load, views, results):
        shifted, loss, slope, second_now = views
        grad_now = shifted[...].astype(F32) + loss[...].astype(F32)
        emit(2, grad_now.astype(BF16))
        scaled = (grad_now * slope[...]).astype(BF16)
        emit(1, scaled)
        emit(0, dot(second_now[...], scaled).astype(BF16))

    send, scaleds[1][last], grads[1][last] = call(
        again,
        "again",
        v_in=[shifted, loss, slope, second_now],
        h_out=[slim, slim, slim],
        chain=True,
    )
    started = scaleds[1][last]

    gate_out, second_out, first_out = None, None, None
    for slot in reversed(range(last)):
        tasks = [gate_sums(slot + 1, gate_out), second_sums(slot + 1, second_out)]
        if slot + 2 < slots:
            tasks.append(first_sums(slot + 2, first_out))
        send, started, others = step(1, slot, send, started, tasks)
        (gate_out,), (second_out,) = others[:2]
        if slot + 2 < slots:
            ((first_out,),) = others[2:]

    def prepare_close(emit, load, views, results):
        put_rows(results[0], first_back(sizes, load(0)))
        results[1][...] = load(1)[...]
        results[2][...] = load(2)[...]
        inputs = load(3)
        results[3][...] = jnp.concatenate([inputs[0], inputs[1]], axis=1)

    task = (
        prepare_close,
        [first_of(0), grads[1][0], returns[0][0], (section_inputs, (0,))],
        [square, slim_f32, slim, wide],
        [],
        [],
    )
    (first_now, grad, earlier, hidden), (gate_out,), (second_out,), (first_out,) = merged(
        "window_close",
        [task, gate_sums(0, gate_out), second_sums(0, second_out), first_sums(1, first_out)],
        [started],
    )

    def close(emit, load, views, results):
        received, grad, first_now, earlier, hidden = views
        emit(0, (grad[...] + dot(first_now[...], received[...])).astype(BF16))
        emit(1, first_sum(earlier[...], received[...], hidden[...]))

    emitted, first_out = call(
        close,
        "close",
        v_in=[exchange(send, parts), grad, first_now, earlier, hidden],
        h_out=[slim, (factor_shape, (0, 0))],
        into=[(1, first_out)],
        chain=True,
    )
    return emitted[None], first_out, second_out, gate_out.reshape(gate_scales.shape)


def solution(mesh):
    in_specs = (
        P("section", None, "tensor", None),
        P("section", "tensor", None),
        P(None, "tensor", None),
        P("section", None, "tensor", None, None),
        P("section", None, "tensor", None, None),
        P("section", None, "tensor"),
        P("section"),
    )
    out_specs = (
        P("section", "tensor", None),
        P("section", None, "tensor", None, None),
        P("section", None, "tensor", None, None),
        P("section", None, "tensor"),
    )
    return jax.shard_map(shards, mesh=mesh, in_specs=in_specs, out_specs=out_specs, check_vma=False)
```

```python
import jax
import jax.numpy as jnp
from jax import lax
from jax.experimental import pallas as pl
from jax.experimental.pallas import tpu as pltpu
from jax.sharding import PartitionSpec as P

F32 = jnp.float32
BF16 = jnp.bfloat16


def call(body, name, h_in=(), v_in=(), pins=(), v_out=(), h_out=(), into=(), chain=False):
    vmem = pl.BlockSpec(memory_space=pltpu.VMEM)
    hbm = pl.BlockSpec(memory_space=pltpu.HBM)
    arrays = [item[0] if isinstance(item, tuple) else item for item in h_in]
    places = [item[1] if isinstance(item, tuple) else () for item in h_in]
    shapes = [item[0] if isinstance(item, tuple) else item for item in h_out]
    targets = [item[1] if isinstance(item, tuple) else () for item in h_out]
    loads = [pltpu.VMEM(a.shape[len(p) :], a.dtype) for a, p in zip(arrays, places)]
    stores = [pltpu.VMEM(a.shape[len(p) :], a.dtype) for a, p in zip(shapes, targets)]
    pins = [*pins, *(array for _, array in into)]
    ahead = len(arrays) + len(v_in) + len(pins) - len(into)
    alias = {ahead + k: len(v_out) + number for k, (number, _) in enumerate(into)}
    arrays = [pltpu.with_memory_space_constraint(a, pltpu.HBM) for a in arrays]
    pins = [pltpu.with_memory_space_constraint(a, pltpu.HBM) for a in pins]
    inputs = (*arrays, *v_in, *pins)

    def at(ref, place):
        return ref.at[place] if place else ref

    def kernel(*refs):
        sources, refs = refs[: len(arrays)], refs[len(arrays) :]
        views, refs = refs[: len(v_in)], refs[len(v_in) + len(pins) :]
        results, refs = refs[: len(v_out)], refs[len(v_out) :]
        sinks, refs = refs[: len(shapes)], refs[len(shapes) :]
        loaded, refs = refs[: len(loads)], refs[len(loads) :]
        staged, refs = refs[: len(stores)], refs[len(stores) :]
        in_sems, out_sems, half_sems = refs
        copies = [
            pltpu.make_async_copy(at(source, place), buffer, in_sems.at[number])
            for number, (source, place, buffer) in enumerate(zip(sources, places, loaded))
        ]
        for copy in copies:
            copy.start()
        pending = []

        def emit(number, value=None, ref=None):
            if ref is None:
                ref = staged[number]
            if value is not None:
                ref[...] = value
            copy = pltpu.make_async_copy(ref, at(sinks[number], targets[number]), out_sems.at[number])
            copy.start()
            pending.append(copy)

        def emit_product(number, left, right, chunks):
            size = staged[number].shape[0] // chunks
            for chunk in range(chunks):
                rows = slice(chunk * size, (chunk + 1) * size)
                staged[number][rows, :] = dot(left[rows, :], right[...]).astype(BF16)
                if (chunk + 1) * 2 % chunks == 0:
                    part = (chunk + 1) * 2 // chunks - 1
                    half = slice(part * size * chunks // 2, (part + 1) * size * chunks // 2)
                    copy = pltpu.make_async_copy(
                        staged[number].at[half, :], sinks[number].at[half, :], half_sems.at[part]
                    )
                    copy.start()
                    pending.append(copy)

        emit.product, emit.staged = emit_product, staged

        waited = set()

        def load(number):
            if number not in waited:
                waited.add(number)
                copies[number].wait()
            return loaded[number]

        body(emit, load, views, results)
        for copy in pending:
            copy.wait()

    moved = sum(a.size * a.dtype.itemsize for a in (*arrays, *v_in, *v_out, *shapes))
    moved = moved if chain else 1024
    return pl.pallas_call(
        kernel,
        out_shape=[*v_out, *(pltpu.HBM(a.shape, a.dtype) for a in shapes)],
        in_specs=[hbm] * len(arrays) + [vmem] * len(v_in) + [hbm] * len(pins),
        out_specs=[vmem] * len(v_out) + [hbm] * len(shapes),
        scratch_shapes=[
            *loads,
            *stores,
            pltpu.SemaphoreType.DMA((max(1, len(loads)),)),
            pltpu.SemaphoreType.DMA((max(1, len(stores)),)),
            pltpu.SemaphoreType.DMA((2,)),
        ],
        input_output_aliases=alias,
        name=name,
        compiler_params=pltpu.CompilerParams(vmem_limit_bytes=16 << 20),
        cost_estimate=pl.CostEstimate(flops=0, bytes_accessed=moved, transcendentals=0),
    )(*inputs)


def merged(name, tasks, pins=()):
    sources, keys, plans = [], {}, []
    v_out, h_out, into = [], [], []
    for body, needs, shows, keeps, fills in tasks:
        numbers = []
        for item in needs:
            array, place = item if isinstance(item, tuple) else (item, ())
            key = (id(array), place)
            if key not in keys:
                keys[key] = len(sources)
                sources.append((array, place))
            numbers.append(keys[key])
        plans.append((body, numbers, len(v_out), len(h_out)))
        into += [(number + len(h_out), array) for number, array in fills]
        v_out += shows
        h_out += keeps

    def kernel(emit, load, views, results):
        for body, numbers, shown, kept in plans:
            body(
                lambda number, value: emit(kept + number, value),
                lambda number: load(numbers[number]),
                views,
                results[shown:],
            )

    outs = call(kernel, name, h_in=sources, pins=pins, v_out=v_out, h_out=h_out, into=into)
    split = []
    for (_, _, shown, kept), (_, _, shows, keeps, _) in zip(plans, tasks):
        base = len(v_out) + kept
        split.append([*outs[shown : shown + len(shows)], *outs[base : base + len(keeps)]])
    return split


def dot(left, right):
    return jnp.dot(left, right, preferred_element_type=F32)


def dot_t(left, right):
    return lax.dot_general(left, right, (((1,), (1,)), ((), ())), preferred_element_type=F32)


def one_hot(match):
    return jnp.where(match, 1.0, 0.0).astype(BF16)


def first_rows(sizes, axis):
    blocks, size, parts = sizes
    rows = blocks * size
    each = size // parts
    wire = lax.broadcasted_iota(jnp.int32, (rows, rows), axis)
    natural = lax.broadcasted_iota(jnp.int32, (rows, rows), 1 - axis)
    part = wire // (blocks * each)
    block = (wire // each) % blocks
    return one_hot(natural == block * size + part * each + wire % each)


def second_rows(sizes, axis):
    blocks, size, parts = sizes
    rows = blocks * size
    every = blocks * parts
    repeat = size // every
    wire = lax.broadcasted_iota(jnp.int32, (rows, rows), axis)
    natural = lax.broadcasted_iota(jnp.int32, (rows, rows), 1 - axis)
    source = wire // (blocks * repeat)
    block = (wire // repeat) % blocks
    return one_hot(natural == block * size + (wire % repeat) * every + source)


def sigmoid(values):
    return 1.0 / (1.0 + jnp.exp(-values))


def first_wire(sizes, factor):
    blocks, size, _ = sizes
    order = first_rows(sizes, 0)
    return [
        dot(order[:, block * size : (block + 1) * size], factor[block]).astype(BF16)
        for block in range(blocks)
    ]


def first_back(sizes, factor):
    blocks, size, _ = sizes
    order = first_rows(sizes, 1)
    return [
        dot(
            factor[block].astype(F32).T.astype(BF16), order[block * size : (block + 1) * size]
        ).astype(BF16)
        for block in range(blocks)
    ]


def second_wire(sizes, factor):
    blocks, size, _ = sizes
    order = second_rows(sizes, 1)
    return [
        dot(factor[block], order[block * size : (block + 1) * size]).astype(BF16)
        for block in range(blocks)
    ]


def second_back(sizes, factor):
    blocks, size, _ = sizes
    order = second_rows(sizes, 0)
    return [
        dot(
            order[:, block * size : (block + 1) * size], factor[block].astype(F32).T.astype(BF16)
        ).astype(BF16)
        for block in range(blocks)
    ]


def put_rows(ref, parts):
    size = parts[0].shape[0]
    for number, part in enumerate(parts):
        ref[number * size : (number + 1) * size, :] = part


def put_columns(ref, parts):
    size = parts[0].shape[1]
    for number, part in enumerate(parts):
        ref[:, number * size : (number + 1) * size] = part


def column(row, lanes):
    return jnp.broadcast_to(row, (lanes, row.shape[1])).T


def both(value):
    return jnp.concatenate([value, value], axis=1)


def branch_of(mixed):
    return mixed * sigmoid(mixed)


def slope_of(mixed, gates):
    logistic = sigmoid(mixed)
    return gates * logistic * (1.0 + mixed * (1.0 - logistic))


def exchange(values, parts):
    rows, columns = values.shape
    shaped = values.reshape(parts, rows // parts, columns)
    return lax.all_to_all(shaped, "tensor", 0, 0, tiled=True).reshape(rows, columns)


def shards(
    section_inputs, arriving_grad, loss_grad, factor_first, factor_second, gate_scales, layer_count
):
    slots, blocks, size = factor_first.shape[1:4]
    tokens = section_inputs.shape[3]
    parts = lax.axis_size("tensor")
    sizes = (blocks, size, parts)
    rows = blocks * size
    live = jnp.arange(slots) < layer_count[0]
    gate = jnp.where(live[:, None], gate_scales[0], 0.0)[:, None]
    alive = jnp.where(live[:, None], jnp.ones_like(gate_scales[0]), 0.0)[:, None]
    sections = lax.axis_size("section")
    is_last = lax.axis_index("section") == sections - 1
    loss = jnp.where(is_last, loss_grad[0], jnp.zeros_like(loss_grad[0]))
    last = slots - 1

    def shape(columns, dtype=BF16):
        return jax.ShapeDtypeStruct((rows, columns), dtype)

    wide, slim, square = shape(2 * tokens), shape(tokens), shape(rows)
    wide_f32, slim_f32 = shape(2 * tokens, F32), shape(tokens, F32)
    factor_shape = jax.ShapeDtypeStruct(factor_first.shape, BF16)

    def first_of(slot):
        return (factor_first, (0, slot))

    def second_of(slot):
        return (factor_second, (0, slot))

    def gate_of(slot):
        return (gate, (slot,))

    def open_chain(emit, load, views, results):
        order = first_rows(sizes, 0)
        factor, inputs = load(0), load(1)
        hidden = jnp.concatenate([inputs[0], inputs[1]], axis=1)
        natural = jnp.concatenate(
            [
                dot(factor[block], hidden[block * size : (block + 1) * size]).astype(BF16)
                for block in range(blocks)
            ],
            axis=0,
        )
        emit.product(0, order, natural, blocks)

    (send,) = call(
        open_chain, "open", h_in=[first_of(0), (section_inputs, (0,))], h_out=[wide], chain=True
    )
    started = section_inputs

    wires, hiddens, mixeds = [], [], []
    for slot in range(last):

        def prepare(emit, load, views, results, slot=slot):
            put_rows(results[0], second_wire(sizes, load(0)))
            put_columns(results[1], first_wire(sizes, load(1)))
            results[2][...] = column(load(2)[...], tokens)
            before = load(3)
            if slot == 0:
                results[3][...] = jnp.concatenate([before[0], before[1]], axis=1)
            else:
                results[3][...] = before[...]

        second_now, first_now, gate_now, hidden = call(
            prepare,
            f"prepare_forward_{slot}",
            h_in=[
                second_of(slot),
                first_of(slot + 1),
                gate_of(slot),
                (section_inputs, (0,)) if slot == 0 else hiddens[-1],
            ],
            pins=[started],
            v_out=[square, square, slim_f32, wide],
        )

        def forward(emit, load, views, results):
            received, hidden, gate_now, second_now, first_now = views
            emit(1, None, received)
            mixed, fresh = emit.staged[2], emit.staged[3]
            for block in range(blocks):
                span = slice(block * size, (block + 1) * size)
                mixed_now = dot(second_now[span, :], received[...])
                mixed[span, :] = mixed_now
                gates = both(gate_now[span, :])
                fresh[span, :] = (
                    hidden[span, :].astype(F32) + gates * branch_of(mixed_now)
                ).astype(BF16)
            emit(2)
            emit(3)
            emit.product(0, first_now, fresh, blocks)

        send, wire, mixed, fresh = call(
            forward,
            f"forward_{slot}",
            v_in=[exchange(send, parts), hidden, gate_now, second_now, first_now],
            h_out=[wide, wide, wide_f32, wide],
            chain=True,
        )
        wires.append(wire)
        mixeds.append(mixed)
        hiddens.append(fresh)
        started = fresh

    def prepare_turn(emit, load, views, results):
        second = load(0)
        put_rows(results[0], second_wire(sizes, second))
        put_columns(results[1], second_back(sizes, second))
        results[2][...] = column(load(1)[...], tokens)
        results[3][...] = load(2)[...]

    second_now, back_now, gate_now, arriving = call(
        prepare_turn,
        "prepare_turn",
        h_in=[second_of(last), gate_of(last), (arriving_grad, (0,))],
        pins=[started],
        v_out=[square, square, slim_f32, slim],
    )

    def turn(emit, load, views, results):
        received, arriving, gate_now, second_now, back_now = views
        emit(1, None, received)
        mixed, scaled = emit.staged[2], emit.staged[3]
        for block in range(blocks):
            span = slice(block * size, (block + 1) * size)
            mixed_now = dot(second_now[span, :], received[...])
            mixed[span, :] = mixed_now
            slope = slope_of(mixed_now[:, :tokens], gate_now[span, :])
            scaled[span, :] = (arriving[span, :].astype(F32) * slope).astype(BF16)
        emit(2)
        emit(3)
        emit.product(0, back_now, scaled, blocks)

    send, wire, mixed, scaled = call(
        turn,
        "turn",
        v_in=[exchange(send, parts), arriving, gate_now, second_now, back_now],
        h_out=[slim, wide, wide_f32, slim],
        chain=True,
    )
    wires.append(wire)
    mixeds.append(mixed)
    started = scaled

    scaleds = [[None] * slots, [None] * slots]
    grads = [[None] * slots, [None] * slots]
    returns = [[None] * slots, [None] * slots]
    scaleds[0][last], grads[0][last] = scaled, (arriving_grad, (0,))
    gate_shape = jax.ShapeDtypeStruct(gate.shape, F32)

    def gate_sums(slot, filled):
        def body(emit, load, views, results):
            branch = branch_of(load(0)[...])
            terms = load(1)[...].astype(F32) * branch[:, :tokens]
            terms += load(2)[...].astype(F32) * branch[:, tokens:]
            sums = jnp.sum(terms.T, axis=0, keepdims=True)
            emit(0, jnp.where(load(3)[...] > 0, sums, 0.0))

        return (
            body,
            [mixeds[slot], grads[0][slot], grads[1][slot], (alive, (slot,))],
            [],
            [(gate_shape, (slot,))],
            [] if filled is None else [(0, filled)],
        )

    def second_sums(slot, filled):
        def body(emit, load, views, results):
            order = second_rows(sizes, 1)
            natural = dot(order, load(0)[...]).astype(BF16)
            scaled = jnp.concatenate([load(1)[...], load(2)[...]], axis=1)
            sums = []
            for block in range(blocks):
                span = slice(block * size, (block + 1) * size)
                sums.append(dot_t(scaled[span], natural[span]).astype(BF16))
            emit(0, jnp.stack(sums))

        return (
            body,
            [wires[slot], scaleds[0][slot], scaleds[1][slot]],
            [],
            [(factor_shape, (0, slot))],
            [] if filled is None else [(0, filled)],
        )

    def first_sum(earlier, later, hidden):
        wire = jnp.concatenate([earlier, later], axis=1)
        natural = dot(first_rows(sizes, 1), wire).astype(BF16)
        sums = []
        for block in range(blocks):
            span = slice(block * size, (block + 1) * size)
            sums.append(dot_t(natural[span], hidden[span]).astype(BF16))
        return jnp.stack(sums)

    def first_sums(slot, filled):
        def body(emit, load, views, results):
            emit(0, first_sum(load(0)[...], load(1)[...], load(2)[...]))

        return (
            body,
            [returns[0][slot], returns[1][slot], hiddens[slot - 1]],
            [],
            [(factor_shape, (0, slot))],
            [] if filled is None else [(0, filled)],
        )

    def step(moment, slot, send, started, tasks=()):
        columns = slice(moment * tokens, (moment + 1) * tokens)
        kept = BF16 if slot + 1 == last else F32

        def prepare(emit, load, views, results):
            put_rows(results[0], first_back(sizes, load(0)))
            put_columns(results[1], second_back(sizes, load(1)))
            gates = column(load(2)[...], tokens)
            results[2][...] = slope_of(load(3)[:, columns], gates)
            results[3][...] = load(4)[...]

        task = (
            prepare,
            [
                first_of(slot + 1),
                second_of(slot),
                gate_of(slot),
                mixeds[slot],
                grads[moment][slot + 1],
            ],
            [square, square, slim_f32, shape(tokens, kept)],
            [],
            [],
        )
        ready, *others = merged(f"window_{moment}_{slot}", [task, *tasks], [started])
        first_now, second_now, slope, grad = ready

        def backward(emit, load, views, results):
            received, grad, slope, first_now, second_now = views
            emit(1, None, received)
            scaled, grad_out = emit.staged[2], emit.staged[3]
            for block in range(blocks):
                span = slice(block * size, (block + 1) * size)
                grad_now = grad[span, :].astype(F32) + dot(first_now[span, :], received[...])
                grad_out[span, :] = grad_now
                scaled[span, :] = (grad_now * slope[span, :]).astype(BF16)
            emit(3)
            emit(2)
            emit.product(0, second_now, scaled, blocks)

        send, returned, scaled, grad = call(
            backward,
            f"backward_{moment}_{slot}",
            v_in=[exchange(send, parts), grad, slope, first_now, second_now],
            h_out=[slim, slim, slim, slim_f32],
            chain=True,
        )
        returns[moment][slot + 1] = returned
        scaleds[moment][slot] = scaled
        grads[moment][slot] = grad
        return send, scaled, others

    for slot in reversed(range(last)):
        send, started, _ = step(0, slot, send, started)

    def prepare_emit(emit, load, views, results):
        put_rows(results[0], first_back(sizes, load(0)))
        results[1][...] = load(1)[...]

    def prepare_again(emit, load, views, results):
        put_columns(results[0], second_back(sizes, load(0)))
        gates = column(load(1)[...], tokens)
        results[1][...] = slope_of(load(2)[:, tokens:], gates)
        results[2][...] = load(3)[...]

    (first_now, grad), (second_now, slope, loss) = merged(
        "window_emit",
        [
            (prepare_emit, [first_of(0), grads[0][0]], [square, slim_f32], [], []),
            (
                prepare_again,
                [second_of(last), gate_of(last), mixeds[last], loss],
                [square, slim_f32, slim],
                [],
                [],
            ),
        ],
        [started],
    )

    def emit_grad(emit, load, views, results):
        received, grad, first_now = views[:3]
        results[0][...] = (grad[...] + dot(first_now[...], received[...])).astype(BF16)

    returned = exchange(send, parts)
    (emitted,) = call(
        emit_grad, "emit", v_in=[returned, grad, first_now, loss], v_out=[slim], chain=True
    )
    shifted = lax.ppermute(
        emitted, "section", [(source, source - 1) for source in range(1, sections)]
    )

    def again(emit, load, views, results):
        shifted, loss, slope, second_now, returned = views
        emit(3, None, returned)
        grad_now = shifted[...].astype(F32) + loss[...].astype(F32)
        emit(2, grad_now.astype(BF16))
        emit(1, (grad_now * slope[...]).astype(BF16))
        emit.product(0, second_now, emit.staged[1], blocks)

    send, scaleds[1][last], grads[1][last], returns[0][0] = call(
        again,
        "again",
        v_in=[shifted, loss, slope, second_now, returned],
        h_out=[slim, slim, slim, slim],
        chain=True,
    )
    started = scaleds[1][last]

    gate_out, second_out, first_out = None, None, None
    for slot in reversed(range(last)):
        tasks = [gate_sums(slot + 1, gate_out), second_sums(slot + 1, second_out)]
        if slot + 2 < slots:
            tasks.append(first_sums(slot + 2, first_out))
        send, started, others = step(1, slot, send, started, tasks)
        (gate_out,), (second_out,) = others[:2]
        if slot + 2 < slots:
            ((first_out,),) = others[2:]

    def prepare_close(emit, load, views, results):
        put_rows(results[0], first_back(sizes, load(0)))
        results[1][...] = load(1)[...]
        order = first_rows(sizes, 1)
        results[2][...] = order
        inputs = load(3)
        results[3][...] = inputs[1]
        natural = dot(order, load(2)[...]).astype(BF16)
        for block in range(blocks):
            span = slice(block * size, (block + 1) * size)
            results[4][span, :] = dot_t(natural[span], inputs[0, span, :])

    task = (
        prepare_close,
        [first_of(0), grads[1][0], returns[0][0], (section_inputs, (0,))],
        [square, slim_f32, square, slim, shape(size, F32)],
        [],
        [],
    )
    (first_now, grad, order, hidden, sums), (gate_out,), (second_out,), (first_out,) = merged(
        "window_close",
        [task, gate_sums(0, gate_out), second_sums(0, second_out), first_sums(1, first_out)],
        [started],
    )

    def close(emit, load, views, results):
        received, grad, first_now, order, hidden, sums = views
        factor_out = emit.staged[1]
        natural = dot(order[...], received[...]).astype(BF16)
        emit(0, (grad[...] + dot(first_now[...], received[...])).astype(BF16))
        for block in range(blocks):
            span = slice(block * size, (block + 1) * size)
            factor_out[block] = (sums[span, :] + dot_t(natural[span], hidden[span, :])).astype(BF16)
        emit(1)

    emitted, first_out = call(
        close,
        "close",
        v_in=[exchange(send, parts), grad, first_now, order, hidden, sums],
        h_out=[slim, (factor_shape, (0, 0))],
        into=[(1, first_out)],
        chain=True,
    )
    return emitted[None], first_out, second_out, gate_out.reshape(gate_scales.shape)


def solution(mesh):
    in_specs = (
        P("section", None, "tensor", None),
        P("section", "tensor", None),
        P(None, "tensor", None),
        P("section", None, "tensor", None, None),
        P("section", None, "tensor", None, None),
        P("section", None, "tensor"),
        P("section"),
    )
    out_specs = (
        P("section", "tensor", None),
        P("section", None, "tensor", None, None),
        P("section", None, "tensor", None, None),
        P("section", None, "tensor"),
    )
    return jax.shard_map(shards, mesh=mesh, in_specs=in_specs, out_specs=out_specs, check_vma=False)
```

```python
import jax
import jax.numpy as jnp
from jax import lax
from jax.experimental import pallas as pl
from jax.experimental.pallas import tpu as pltpu
from jax.sharding import PartitionSpec as P

F32 = jnp.float32
BF16 = jnp.bfloat16


def call(body, name, h_in=(), v_in=(), pins=(), v_out=(), h_out=(), into=(), chain=False):
    vmem = pl.BlockSpec(memory_space=pltpu.VMEM)
    hbm = pl.BlockSpec(memory_space=pltpu.HBM)
    arrays = [item[0] if isinstance(item, tuple) else item for item in h_in]
    places = [item[1] if isinstance(item, tuple) else () for item in h_in]
    shapes = [item[0] if isinstance(item, tuple) else item for item in h_out]
    targets = [item[1] if isinstance(item, tuple) else () for item in h_out]
    loads = [pltpu.VMEM(a.shape[len(p) :], a.dtype) for a, p in zip(arrays, places)]
    stores = [pltpu.VMEM(a.shape[len(p) :], a.dtype) for a, p in zip(shapes, targets)]
    pins = [*pins, *(array for _, array in into)]
    ahead = len(arrays) + len(v_in) + len(pins) - len(into)
    alias = {ahead + k: len(v_out) + number for k, (number, _) in enumerate(into)}
    arrays = [pltpu.with_memory_space_constraint(a, pltpu.HBM) for a in arrays]
    pins = [pltpu.with_memory_space_constraint(a, pltpu.HBM) for a in pins]
    inputs = (*arrays, *v_in, *pins)

    def at(ref, place):
        return ref.at[place] if place else ref

    def kernel(*refs):
        sources, refs = refs[: len(arrays)], refs[len(arrays) :]
        views, refs = refs[: len(v_in)], refs[len(v_in) + len(pins) :]
        results, refs = refs[: len(v_out)], refs[len(v_out) :]
        sinks, refs = refs[: len(shapes)], refs[len(shapes) :]
        loaded, refs = refs[: len(loads)], refs[len(loads) :]
        staged, refs = refs[: len(stores)], refs[len(stores) :]
        in_sems, out_sems, half_sems = refs
        copies = [
            pltpu.make_async_copy(at(source, place), buffer, in_sems.at[number])
            for number, (source, place, buffer) in enumerate(zip(sources, places, loaded))
        ]
        for copy in copies:
            copy.start()
        pending = []

        def emit(number, value=None, ref=None):
            if ref is None:
                ref = staged[number]
            if value is not None:
                ref[...] = value
            copy = pltpu.make_async_copy(ref, at(sinks[number], targets[number]), out_sems.at[number])
            copy.start()
            pending.append(copy)

        def emit_product(number, left, right, chunks):
            size = staged[number].shape[0] // chunks
            for chunk in range(chunks):
                rows = slice(chunk * size, (chunk + 1) * size)
                staged[number][rows, :] = dot(left[rows, :], right[...]).astype(BF16)
                if (chunk + 1) * 2 % chunks == 0:
                    part = (chunk + 1) * 2 // chunks - 1
                    half = slice(part * size * chunks // 2, (part + 1) * size * chunks // 2)
                    copy = pltpu.make_async_copy(
                        staged[number].at[half, :], sinks[number].at[half, :], half_sems.at[part]
                    )
                    copy.start()
                    pending.append(copy)

        emit.product, emit.staged = emit_product, staged

        waited = set()

        def load(number):
            if number not in waited:
                waited.add(number)
                copies[number].wait()
            return loaded[number]

        body(emit, load, views, results)
        for copy in pending:
            copy.wait()

    moved = sum(a.size * a.dtype.itemsize for a in (*arrays, *v_in, *v_out, *shapes))
    moved = moved if chain else 1024
    return pl.pallas_call(
        kernel,
        out_shape=[*v_out, *(pltpu.HBM(a.shape, a.dtype) for a in shapes)],
        in_specs=[hbm] * len(arrays) + [vmem] * len(v_in) + [hbm] * len(pins),
        out_specs=[vmem] * len(v_out) + [hbm] * len(shapes),
        scratch_shapes=[
            *loads,
            *stores,
            pltpu.SemaphoreType.DMA((max(1, len(loads)),)),
            pltpu.SemaphoreType.DMA((max(1, len(stores)),)),
            pltpu.SemaphoreType.DMA((2,)),
        ],
        input_output_aliases=alias,
        name=name,
        compiler_params=pltpu.CompilerParams(vmem_limit_bytes=16 << 20),
        cost_estimate=pl.CostEstimate(flops=0, bytes_accessed=moved, transcendentals=0),
    )(*inputs)


def merged(name, tasks, pins=()):
    sources, keys, plans = [], {}, []
    v_out, h_out, into = [], [], []
    for body, needs, shows, keeps, fills in tasks:
        numbers = []
        for item in needs:
            array, place = item if isinstance(item, tuple) else (item, ())
            key = (id(array), place)
            if key not in keys:
                keys[key] = len(sources)
                sources.append((array, place))
            numbers.append(keys[key])
        plans.append((body, numbers, len(v_out), len(h_out)))
        into += [(number + len(h_out), array) for number, array in fills]
        v_out += shows
        h_out += keeps

    def kernel(emit, load, views, results):
        for body, numbers, shown, kept in plans:
            body(
                lambda number, value: emit(kept + number, value),
                lambda number: load(numbers[number]),
                views,
                results[shown:],
            )

    outs = call(kernel, name, h_in=sources, pins=pins, v_out=v_out, h_out=h_out, into=into)
    split = []
    for (_, _, shown, kept), (_, _, shows, keeps, _) in zip(plans, tasks):
        base = len(v_out) + kept
        split.append([*outs[shown : shown + len(shows)], *outs[base : base + len(keeps)]])
    return split


def dot(left, right):
    return jnp.dot(left, right, preferred_element_type=F32)


def dot_t(left, right):
    return lax.dot_general(left, right, (((1,), (1,)), ((), ())), preferred_element_type=F32)


def one_hot(match):
    return jnp.where(match, 1.0, 0.0).astype(BF16)


def first_rows(sizes, axis):
    blocks, size, parts = sizes
    rows = blocks * size
    each = size // parts
    wire = lax.broadcasted_iota(jnp.int32, (rows, rows), axis)
    natural = lax.broadcasted_iota(jnp.int32, (rows, rows), 1 - axis)
    part = wire // (blocks * each)
    block = (wire // each) % blocks
    return one_hot(natural == block * size + part * each + wire % each)


def second_rows(sizes, axis):
    blocks, size, parts = sizes
    rows = blocks * size
    every = blocks * parts
    repeat = size // every
    wire = lax.broadcasted_iota(jnp.int32, (rows, rows), axis)
    natural = lax.broadcasted_iota(jnp.int32, (rows, rows), 1 - axis)
    source = wire // (blocks * repeat)
    block = (wire // repeat) % blocks
    return one_hot(natural == block * size + (wire % repeat) * every + source)


def sigmoid(values):
    return 1.0 / (1.0 + jnp.exp(-values))


def first_wire(sizes, factor):
    blocks, size, _ = sizes
    order = first_rows(sizes, 0)
    return [
        dot(order[:, block * size : (block + 1) * size], factor[block]).astype(BF16)
        for block in range(blocks)
    ]


def first_back(sizes, factor):
    blocks, size, _ = sizes
    order = first_rows(sizes, 1)
    return [
        dot(
            factor[block].astype(F32).T.astype(BF16), order[block * size : (block + 1) * size]
        ).astype(BF16)
        for block in range(blocks)
    ]


def second_wire(sizes, factor):
    blocks, size, _ = sizes
    order = second_rows(sizes, 1)
    return [
        dot(factor[block], order[block * size : (block + 1) * size]).astype(BF16)
        for block in range(blocks)
    ]


def second_back(sizes, factor):
    blocks, size, _ = sizes
    order = second_rows(sizes, 0)
    return [
        dot(
            order[:, block * size : (block + 1) * size], factor[block].astype(F32).T.astype(BF16)
        ).astype(BF16)
        for block in range(blocks)
    ]


def put_rows(ref, parts):
    size = parts[0].shape[0]
    for number, part in enumerate(parts):
        ref[number * size : (number + 1) * size, :] = part


def put_columns(ref, parts):
    size = parts[0].shape[1]
    for number, part in enumerate(parts):
        ref[:, number * size : (number + 1) * size] = part


def column(row, lanes):
    return jnp.broadcast_to(row, (lanes, row.shape[1])).T


def both(value):
    return jnp.concatenate([value, value], axis=1)


def branch_of(mixed):
    return mixed * sigmoid(mixed)


def slope_of(mixed, gates):
    logistic = sigmoid(mixed)
    return gates * logistic * (1.0 + mixed * (1.0 - logistic))


def exchange(values, parts):
    rows, columns = values.shape
    shaped = values.reshape(parts, rows // parts, columns)
    return lax.all_to_all(shaped, "tensor", 0, 0, tiled=True).reshape(rows, columns)


def shards(
    section_inputs, arriving_grad, loss_grad, factor_first, factor_second, gate_scales, layer_count
):
    slots, blocks, size = factor_first.shape[1:4]
    tokens = section_inputs.shape[3]
    parts = lax.axis_size("tensor")
    sizes = (blocks, size, parts)
    rows = blocks * size
    live = jnp.arange(slots) < layer_count[0]
    gate = jnp.where(live[:, None], gate_scales[0], 0.0)[:, None]
    alive = jnp.where(live[:, None], jnp.ones_like(gate_scales[0]), 0.0)[:, None]
    sections = lax.axis_size("section")
    is_last = lax.axis_index("section") == sections - 1
    loss = jnp.where(is_last, loss_grad[0], jnp.zeros_like(loss_grad[0]))
    last = slots - 1

    def shape(columns, dtype=BF16):
        return jax.ShapeDtypeStruct((rows, columns), dtype)

    wide, slim, square = shape(2 * tokens), shape(tokens), shape(rows)
    slim_f32 = shape(tokens, F32)
    factor_shape = jax.ShapeDtypeStruct(factor_first.shape, BF16)

    def first_of(slot):
        return (factor_first, (0, slot))

    def second_of(slot):
        return (factor_second, (0, slot))

    def gate_of(slot):
        return (gate, (slot,))

    def open_chain(emit, load, views, results):
        order = first_rows(sizes, 0)
        factor, inputs = load(0), load(1)
        hidden = jnp.concatenate([inputs[0], inputs[1]], axis=1)
        natural = jnp.concatenate(
            [
                dot(factor[block], hidden[block * size : (block + 1) * size]).astype(BF16)
                for block in range(blocks)
            ],
            axis=0,
        )
        emit.product(0, order, natural, blocks)

    (send,) = call(
        open_chain, "open", h_in=[first_of(0), (section_inputs, (0,))], h_out=[wide], chain=True
    )
    started = section_inputs

    wires, hiddens, mixeds = [], [], []
    for slot in range(last):

        def prepare(emit, load, views, results, slot=slot):
            put_rows(results[0], second_wire(sizes, load(0)))
            put_columns(results[1], first_wire(sizes, load(1)))
            results[2][...] = column(load(2)[...], tokens)
            before = load(3)
            if slot == 0:
                results[3][...] = jnp.concatenate([before[0], before[1]], axis=1)
            else:
                results[3][...] = before[...]

        second_now, first_now, gate_now, hidden = call(
            prepare,
            f"prepare_forward_{slot}",
            h_in=[
                second_of(slot),
                first_of(slot + 1),
                gate_of(slot),
                (section_inputs, (0,)) if slot == 0 else hiddens[-1],
            ],
            pins=[started],
            v_out=[square, square, slim_f32, wide],
        )

        def forward(emit, load, views, results):
            received, hidden, gate_now, second_now, first_now = views
            emit(1, None, received)
            mixed, fresh, mixed_later = emit.staged[2], emit.staged[3], emit.staged[4]
            for block in range(blocks):
                span = slice(block * size, (block + 1) * size)
                mixed_now = dot(second_now[span, :], received[...])
                mixed[span, :] = mixed_now[:, :tokens]
                mixed_later[span, :] = mixed_now[:, tokens:]
                gates = both(gate_now[span, :])
                fresh[span, :] = (
                    hidden[span, :].astype(F32) + gates * branch_of(mixed_now)
                ).astype(BF16)
            emit(2)
            emit(4)
            emit(3)
            emit.product(0, first_now, fresh, blocks)

        send, wire, mixed, fresh, mixed_later = call(
            forward,
            f"forward_{slot}",
            v_in=[exchange(send, parts), hidden, gate_now, second_now, first_now],
            h_out=[wide, wide, slim_f32, wide, slim_f32],
            chain=True,
        )
        wires.append(wire)
        mixeds.append((mixed, mixed_later))
        hiddens.append(fresh)
        started = fresh

    def prepare_turn(emit, load, views, results):
        second = load(0)
        put_rows(results[0], second_wire(sizes, second))
        put_columns(results[1], second_back(sizes, second))
        results[2][...] = column(load(1)[...], tokens)
        results[3][...] = load(2)[...]

    second_now, back_now, gate_now, arriving = call(
        prepare_turn,
        "prepare_turn",
        h_in=[second_of(last), gate_of(last), (arriving_grad, (0,))],
        pins=[started],
        v_out=[square, square, slim_f32, slim],
    )

    def turn(emit, load, views, results):
        received, arriving, gate_now, second_now, back_now = views
        emit(1, None, received)
        mixed, scaled, mixed_later = emit.staged[2], emit.staged[3], emit.staged[4]
        for block in range(blocks):
            span = slice(block * size, (block + 1) * size)
            mixed_now = dot(second_now[span, :], received[...])
            mixed[span, :] = mixed_now[:, :tokens]
            mixed_later[span, :] = mixed_now[:, tokens:]
            slope = slope_of(mixed_now[:, :tokens], gate_now[span, :])
            scaled[span, :] = (arriving[span, :].astype(F32) * slope).astype(BF16)
        emit(2)
        emit(4)
        emit(3)
        emit.product(0, back_now, scaled, blocks)

    send, wire, mixed, scaled, mixed_later = call(
        turn,
        "turn",
        v_in=[exchange(send, parts), arriving, gate_now, second_now, back_now],
        h_out=[slim, wide, slim_f32, slim, slim_f32],
        chain=True,
    )
    wires.append(wire)
    mixeds.append((mixed, mixed_later))
    started = scaled

    scaleds = [[None] * slots, [None] * slots]
    grads = [[None] * slots, [None] * slots]
    returns = [[None] * slots, [None] * slots]
    scaleds[0][last], grads[0][last] = scaled, (arriving_grad, (0,))
    gate_shape = jax.ShapeDtypeStruct(gate.shape, F32)

    gate_parts = [None] * slots

    def gate_terms(load):
        terms = load(1)[...].astype(F32) * branch_of(load(0)[...])
        return jnp.sum(terms.T, axis=0, keepdims=True)

    def gate_first(slot):
        def body(emit, load, views, results):
            emit(0, gate_terms(load))

        return (
            body,
            [mixeds[slot][0], grads[0][slot]],
            [],
            [jax.ShapeDtypeStruct((1, rows), F32)],
            [],
        )

    def gate_sums(slot, filled):
        def body(emit, load, views, results):
            sums = load(3)[...] + gate_terms(load)
            emit(0, jnp.where(load(2)[...] > 0, sums, 0.0))

        return (
            body,
            [mixeds[slot][1], grads[1][slot], (alive, (slot,)), gate_parts[slot]],
            [],
            [(gate_shape, (slot,))],
            [] if filled is None else [(0, filled)],
        )

    def second_sums(slot, filled):
        def body(emit, load, views, results):
            order = second_rows(sizes, 1)
            natural = dot(order, load(0)[...]).astype(BF16)
            scaled = jnp.concatenate([load(1)[...], load(2)[...]], axis=1)
            sums = []
            for block in range(blocks):
                span = slice(block * size, (block + 1) * size)
                sums.append(dot_t(scaled[span], natural[span]).astype(BF16))
            emit(0, jnp.stack(sums))

        return (
            body,
            [wires[slot], scaleds[0][slot], scaleds[1][slot]],
            [],
            [(factor_shape, (0, slot))],
            [] if filled is None else [(0, filled)],
        )

    def first_sum(earlier, later, hidden):
        wire = jnp.concatenate([earlier, later], axis=1)
        natural = dot(first_rows(sizes, 1), wire).astype(BF16)
        sums = []
        for block in range(blocks):
            span = slice(block * size, (block + 1) * size)
            sums.append(dot_t(natural[span], hidden[span]).astype(BF16))
        return jnp.stack(sums)

    def first_sums(slot, filled):
        def body(emit, load, views, results):
            emit(0, first_sum(load(0)[...], load(1)[...], load(2)[...]))

        return (
            body,
            [returns[0][slot], returns[1][slot], hiddens[slot - 1]],
            [],
            [(factor_shape, (0, slot))],
            [] if filled is None else [(0, filled)],
        )

    def step(moment, slot, send, started, tasks=()):
        kept = BF16 if slot + 1 == last else F32

        def prepare(emit, load, views, results):
            put_rows(results[0], first_back(sizes, load(0)))
            put_columns(results[1], second_back(sizes, load(1)))
            gates = column(load(2)[...], tokens)
            results[2][...] = slope_of(load(3)[...], gates)
            results[3][...] = load(4)[...]

        task = (
            prepare,
            [
                first_of(slot + 1),
                second_of(slot),
                gate_of(slot),
                mixeds[slot][moment],
                grads[moment][slot + 1],
            ],
            [square, square, slim_f32, shape(tokens, kept)],
            [],
            [],
        )
        ready, *others = merged(f"window_{moment}_{slot}", [task, *tasks], [started])
        first_now, second_now, slope, grad = ready

        def backward(emit, load, views, results):
            received, grad, slope, first_now, second_now = views
            emit(1, None, received)
            scaled, grad_out = emit.staged[2], emit.staged[3]
            for block in range(blocks):
                span = slice(block * size, (block + 1) * size)
                grad_now = grad[span, :].astype(F32) + dot(first_now[span, :], received[...])
                grad_out[span, :] = grad_now
                scaled[span, :] = (grad_now * slope[span, :]).astype(BF16)
            emit(3)
            emit(2)
            emit.product(0, second_now, scaled, blocks)

        send, returned, scaled, grad = call(
            backward,
            f"backward_{moment}_{slot}",
            v_in=[exchange(send, parts), grad, slope, first_now, second_now],
            h_out=[slim, slim, slim, slim_f32],
            chain=True,
        )
        returns[moment][slot + 1] = returned
        scaleds[moment][slot] = scaled
        grads[moment][slot] = grad
        return send, scaled, others

    for slot in reversed(range(last)):
        send, started, others = step(0, slot, send, started, [gate_first(slot + 1)])
        ((gate_parts[slot + 1],),) = others

    def prepare_emit(emit, load, views, results):
        put_rows(results[0], first_back(sizes, load(0)))
        results[1][...] = load(1)[...]

    def prepare_again(emit, load, views, results):
        put_columns(results[0], second_back(sizes, load(0)))
        gates = column(load(1)[...], tokens)
        results[1][...] = slope_of(load(2)[...], gates)
        results[2][...] = load(3)[...]

    (first_now, grad), (second_now, slope, loss), (gate_parts[0],) = merged(
        "window_emit",
        [
            (prepare_emit, [first_of(0), grads[0][0]], [square, slim_f32], [], []),
            (
                prepare_again,
                [second_of(last), gate_of(last), mixeds[last][1], loss],
                [square, slim_f32, slim],
                [],
                [],
            ),
            gate_first(0),
        ],
        [started],
    )

    def emit_grad(emit, load, views, results):
        received, grad, first_now = views[:3]
        results[0][...] = (grad[...] + dot(first_now[...], received[...])).astype(BF16)

    returned = exchange(send, parts)
    (emitted,) = call(
        emit_grad, "emit", v_in=[returned, grad, first_now, loss], v_out=[slim], chain=True
    )
    shifted = lax.ppermute(
        emitted, "section", [(source, source - 1) for source in range(1, sections)]
    )

    def again(emit, load, views, results):
        shifted, loss, slope, second_now, returned = views
        emit(3, None, returned)
        grad_now = shifted[...].astype(F32) + loss[...].astype(F32)
        emit(2, grad_now.astype(BF16))
        emit(1, (grad_now * slope[...]).astype(BF16))
        emit.product(0, second_now, emit.staged[1], blocks)

    send, scaleds[1][last], grads[1][last], returns[0][0] = call(
        again,
        "again",
        v_in=[shifted, loss, slope, second_now, returned],
        h_out=[slim, slim, slim, slim],
        chain=True,
    )
    started = scaleds[1][last]

    gate_out, second_out, first_out = None, None, None
    for slot in reversed(range(last)):
        tasks = [gate_sums(slot + 1, gate_out), second_sums(slot + 1, second_out)]
        if slot + 2 < slots:
            tasks.append(first_sums(slot + 2, first_out))
        send, started, others = step(1, slot, send, started, tasks)
        (gate_out,), (second_out,) = others[:2]
        if slot + 2 < slots:
            ((first_out,),) = others[2:]

    def prepare_close(emit, load, views, results):
        put_rows(results[0], first_back(sizes, load(0)))
        results[1][...] = load(1)[...]
        order = first_rows(sizes, 1)
        results[2][...] = order
        inputs = load(3)
        results[3][...] = inputs[1]
        natural = dot(order, load(2)[...]).astype(BF16)
        for block in range(blocks):
            span = slice(block * size, (block + 1) * size)
            results[4][span, :] = dot_t(natural[span], inputs[0, span, :])

    task = (
        prepare_close,
        [first_of(0), grads[1][0], returns[0][0], (section_inputs, (0,))],
        [square, slim_f32, square, slim, shape(size, F32)],
        [],
        [],
    )
    (first_now, grad, order, hidden, sums), (gate_out,), (second_out,), (first_out,) = merged(
        "window_close",
        [task, gate_sums(0, gate_out), second_sums(0, second_out), first_sums(1, first_out)],
        [started],
    )

    def close(emit, load, views, results):
        received, grad, first_now, order, hidden, sums = views
        factor_out = emit.staged[1]
        natural = dot(order[...], received[...]).astype(BF16)
        emit(0, (grad[...] + dot(first_now[...], received[...])).astype(BF16))
        for block in range(blocks):
            span = slice(block * size, (block + 1) * size)
            factor_out[block] = (sums[span, :] + dot_t(natural[span], hidden[span, :])).astype(BF16)
        emit(1)

    emitted, first_out = call(
        close,
        "close",
        v_in=[exchange(send, parts), grad, first_now, order, hidden, sums],
        h_out=[slim, (factor_shape, (0, 0))],
        into=[(1, first_out)],
        chain=True,
    )
    return emitted[None], first_out, second_out, gate_out.reshape(gate_scales.shape)


def solution(mesh):
    in_specs = (
        P("section", None, "tensor", None),
        P("section", "tensor", None),
        P(None, "tensor", None),
        P("section", None, "tensor", None, None),
        P("section", None, "tensor", None, None),
        P("section", None, "tensor"),
        P("section"),
    )
    out_specs = (
        P("section", "tensor", None),
        P("section", None, "tensor", None, None),
        P("section", None, "tensor", None, None),
        P("section", None, "tensor"),
    )
    return jax.shard_map(shards, mesh=mesh, in_specs=in_specs, out_specs=out_specs, check_vma=False)
```
